128 devices in a mesh: seq: 32 (over x, y, core), ch: 4 (over z).
Axes of the slice: x: 4, y: 4, z: 4, core: 2. Of those that a mesh axis runs over, the one named last changes fastest.
Arguments:
- query_feat: bfloat16 [32768, 4096], P('seq', 'ch'), may hold values from -6 to 6
- key_feat: bfloat16 [32768, 4096], P('seq', 'ch'), may hold values from -6 to 6
- value_feat: bfloat16 [32768, 4096], P('seq', 'ch'), may hold values from -6 to 6
- decay_rates: float32 [256, 16], P('ch'), may hold values from 6.1035156e-06 to 0.041666667
- residues: float32 [256, 16], P('ch'), may hold values from -0.28867513 to 0.28867513
- out_weight: bfloat16 [4096, 4096], P('ch', 'seq'), may hold values from -0.09375 to 0.09375
Outputs:
- mixed: bfloat16 [32768, 4096], P(('seq', 'ch'))
The draws below stay inside these ranges and needn't reach their ends.
All inputs are finite; a program needn't handle non-finite values.
Results may differ from the reference program's by a relative error of at most 0.014.
Values may be sent and summed in bfloat16 or wider, within the bound.
A program may use at most 128 MiB of HBM per device.

```python
import math
import jax
import jax.numpy as jnp
import numpy as np
from jax import lax

D = 4096
MODES = 16
SUB = 256
SEQ_LEN = 32768
GROUPS = 256


def rate_table(key):
    slow_key, fast_key, pick_key = jax.random.split(jax.random.fold_in(key, 11), 3)
    slow = jnp.exp(jax.random.uniform(slow_key, (GROUPS, MODES), jnp.float32, math.log(0.2 / SEQ_LEN), math.log(2.0 / SEQ_LEN)))
    fast = jnp.exp(jax.random.uniform(fast_key, (GROUPS, MODES), jnp.float32, math.log(1.0 / 64), math.log(1.0 / 24)))
    share = 0.5
    picked = jax.random.uniform(pick_key, (GROUPS, MODES), jnp.float32) < share
    return jnp.clip(jnp.where(picked, slow, fast), 0.2 / SEQ_LEN, 1.0 / 24)


def draw_decay_rates(key, part):
    return rate_table(key).astype(jnp.float32)


def draw_residues(key, part):
    table = rate_table(key)
    noise_key = jax.random.fold_in(key, 23)
    noise = jax.random.truncated_normal(noise_key, -4.0, 4.0, (GROUPS, MODES), jnp.float32)
    return (noise * jnp.sqrt(2.0 * table / MODES)).astype(jnp.float32)


def block_levels(own_key, dims, pieces, least, top_value):
    def one(axis_at, parts):
        heights = jax.random.uniform(jax.random.fold_in(jax.random.fold_in(own_key, 6), axis_at), (parts,), jnp.float32, least / len(pieces), top_value / len(pieces))
        return jnp.repeat(jnp.exp(heights), dims[axis_at] // parts).reshape((-1,) + (1,) * (len(dims) - axis_at - 1))

    gain = one(*pieces[0])
    for cut in pieces[1:]:
        gain = gain * one(*cut)
    return gain


def bell_draw(own_key, dims, scale, bound, cuts=(), kind=jnp.bfloat16):
    array = scale * jax.random.normal(own_key, dims, jnp.float32)
    if cuts:
        array = array * block_levels(own_key, dims, cuts, -0.22, 0.18)
    return jnp.clip(array, -bound, bound).astype(kind)


def setup_inputs(seed: int = 0) -> dict:
    arg_keys = jax.random.split(jax.random.key(seed), 7)
    query_feat = bell_draw(arg_keys[0], (SEQ_LEN, D), 1.0, 6.0, ((0, 32), (1, 4)))
    key_feat = bell_draw(arg_keys[1], (SEQ_LEN, D), 1.0, 6.0, ((0, 32), (1, 4)))
    value_feat = bell_draw(arg_keys[2], (SEQ_LEN, D), 1.0, 6.0, ((0, 32), (1, 4)))
    decay_rates = draw_decay_rates(jax.random.fold_in(arg_keys[6], 71), 0)
    residues = draw_residues(jax.random.fold_in(arg_keys[6], 71), 0)
    out_weight = bell_draw(arg_keys[5], (D, D), D ** -0.5, 0.09375, ((0, 4), (1, 32)))
    return {"query_feat": query_feat, "key_feat": key_feat, "value_feat": value_feat, "decay_rates": decay_rates, "residues": residues, "out_weight": out_weight}


def lag_table(block):
    rows = np.arange(block)[:, None]
    cols = np.arange(block)[None, :]
    return rows - cols + block


def reference(query_feat, key_feat, value_feat, decay_rates, residues, out_weight):
    seq_rows, width = query_feat.shape
    group_count, mode_count = decay_rates.shape
    group_width = width // group_count
    block_count = seq_rows // SUB
    hi = lax.Precision.HIGHEST
    mixed_u = (key_feat.astype(jnp.float32) * value_feat.astype(jnp.float32)).astype(jnp.bfloat16)
    lag_steps = jnp.arange(SUB, dtype=jnp.float32)
    filter_taps = jnp.sum(residues[:, :, None] * jnp.exp(-decay_rates[:, :, None] * lag_steps), axis=1).astype(jnp.bfloat16)
    padded = jnp.concatenate([jnp.zeros((group_count, SUB), jnp.bfloat16), filter_taps], axis=1)
    toeplitz = padded[:, lag_table(SUB)].astype(jnp.float32)
    inject = jnp.exp(-decay_rates[:, :, None] * (SUB - 1.0 - lag_steps)).astype(jnp.bfloat16).astype(jnp.float32)
    readout = residues[:, :, None] * jnp.exp(-decay_rates[:, :, None] * (lag_steps + 1.0))
    step_decay = jnp.exp(-decay_rates * SUB).T[:, :, None]
    blocks_u = mixed_u.reshape(block_count, SUB, group_count, group_width)
    blocks_q = query_feat.reshape(block_count, SUB, group_count, group_width)

    def advance(state, inputs):
        block_u, block_q = inputs
        uf = block_u.astype(jnp.float32)
        local_part = jnp.einsum("gab,bgc->agc", toeplitz, uf, precision=hi)
        carried = jnp.einsum("gma,mgc->agc", readout, state, precision=hi)
        gated = (block_q.astype(jnp.float32) * (local_part + carried)).astype(jnp.bfloat16)
        block_sums = jnp.einsum("gmb,bgc->mgc", inject, uf, precision=hi)
        return step_decay * state + block_sums, gated

    start_state = jnp.zeros((mode_count, group_count, group_width), jnp.float32)
    _, gated_all = lax.scan(advance, start_state, (blocks_u, blocks_q))
    gated_all = gated_all.reshape(seq_rows, width)
    return jnp.dot(gated_all, out_weight, preferred_element_type=jnp.float32).astype(jnp.bfloat16)
```

```python
import functools

import jax
import jax.numpy as jnp
from jax import lax
from jax.experimental import pallas as pl
from jax.experimental.pallas import tpu as pltpu
from jax.sharding import PartitionSpec as P

SUB = 256
LANES = 128
TILES = 8
RING = 4
CHIPS = RING * RING
CHUNKS = CHIPS // 2
F32 = jnp.float32
BF16 = jnp.bfloat16
MESH = pl.DeviceIdType.MESH

ORDER = [
    (0, 0), (1, 0), (3, 0), (0, 1), (0, 3), (2, 0), (0, 2), (1, 1),
    (1, 3), (3, 1), (3, 3), (2, 1), (2, 3), (1, 2), (3, 2), (2, 2),
]


def kernel(
    q_hbm, k_hbm, v_hbm, w_hbm, rates_ref, lam_ref, res_ref, taps_ref, out_hbm,
    qb, kb, vb, ub, zloc, band, bs, ent, wb, lhs, send_a, send_b, recv_b, acc, stage,
    st_send, st_sib, st_y, st_x,
    load_sem, sib_sem, st_sem, w_send, w_recv, a_sem, b_sem, fwd_sem, o_sem,
):
    s = lax.axis_index("seq")
    z = lax.axis_index("ch")
    x = lax.div(s, 8)
    y = lax.rem(lax.div(s, 2), 4)
    c = lax.rem(s, 2)
    par = lax.rem(z, 2)
    z_a = z + 1 - 2 * par
    z_b = 3 - z
    sib = s + 1 - 2 * c

    def at_xy(dx, dy):
        return (lax.rem(x + dx, 4) * 4 + lax.rem(y + dy, 4)) * 2 + c

    def chip(dx, dy):
        return lax.rem(x + dx, 4) * 4 + lax.rem(y + dy, 4)

    pending = []

    def remote(src, dst, ssem, rsem, dev):
        return pltpu.make_async_remote_copy(
            src_ref=src, dst_ref=dst, send_sem=ssem, recv_sem=rsem, device_id=dev, device_id_type=MESH
        )

    def send(src, dst, ssem, rsem, dev):
        cp = remote(src, dst, ssem, rsem, dev)
        cp.start()
        pending.append(cp)

    loads = []
    for i, (src, dst) in enumerate(((k_hbm, kb), (v_hbm, vb), (q_hbm, qb))):
        loads.append(pltpu.make_async_copy(src, dst, load_sem.at[i]))
    for r in range(2):
        loads.append(
            pltpu.make_async_copy(w_hbm.at[pl.ds(r * 512, 512), :], wb.at[chip(0, 0), r, par], load_sem.at[3 + r])
        )
    for cp in loads:
        cp.start()

    partners = [(sib, z), (s, z_a), (s, z_b)]
    partners += [(at_xy(d, 0), z) for d in (1, 2, 3)] + [(at_xy(0, d), z) for d in (1, 2, 3)]
    barrier = pltpu.get_barrier_semaphore()
    for dev in partners:
        pl.semaphore_signal(barrier, inc=1, device_id=dev, device_id_type=MESH)
    pl.semaphore_wait(barrier, len(partners))

    own = chip(0, 0)
    for r in range(2):
        send(w_hbm.at[pl.ds(r * 512, 512), :], wb.at[own, r, par], w_send.at[r], w_recv.at[r], (s, z_a))

    send_slots = {}
    recv_slots = {}

    def slot_of(table, base, key):
        if key not in table:
            table[key] = base + len(table)
        return table[key]

    def to_xy(r, df, dg):
        return (df, dg) if r == 0 else (dg, df)

    def w_copy(r, origin, step, half, key):
        slot = chip(*to_xy(r, *origin))
        ref = wb.at[slot, r] if half is None else wb.at[slot, r, half]
        ss = slot_of(send_slots, 2, (r, origin, step, half))
        rs = slot_of(recv_slots, 2, (r,) + key)
        return remote(ref, ref, w_send.at[ss], w_recv.at[rs], (at_xy(*to_xy(r, *step)), z))

    def w_hop(r, origin, step, half):
        key = ((origin[0] - step[0]) % 4, (origin[1] - step[1]) % 4, half)
        cp = w_copy(r, origin, step, half, key)
        cp.start()
        pending.append(cp)

    def w_wait(r, rel, half):
        slot = chip(*to_xy(r, *rel))
        ref = wb.at[slot, r] if half is None else wb.at[slot, r, half]
        rs = slot_of(recv_slots, 2, (r, rel[0], rel[1], half))
        remote(ref, ref, w_send.at[0], w_recv.at[rs], (s, z)).wait_recv()

    arrived = set()

    def arrive(r, rel):
        if (r, rel) in arrived:
            return
        arrived.add((r, rel))
        df, dg = rel
        if rel == (0, 0):
            w_hop(r, rel, (1, 0), None)
            w_hop(r, rel, (3, 0), None)
            w_hop(r, rel, (0, 1), None)
            w_hop(r, rel, (0, 3), None)
            return
        on_f = dg == 0
        d = df if on_f else dg
        if d == 2:
            w_wait(r, rel, 0)
            w_wait(r, rel, 1)
        else:
            w_wait(r, rel, None)
            fwd = 1 if d == 3 else 3
            w_hop(r, rel, (fwd, 0) if on_f else (0, fwd), 0 if d == 3 else 1)
        if on_f:
            w_hop(r, rel, (0, 1), None)
            w_hop(r, rel, (0, 3), None)

    def weights_start():
        for r in range(2):
            loads[3 + r].wait()
            slab = wb.at[own, r, 1 - par]
            remote(slab, slab, w_send.at[0], w_recv.at[r], (s, z_a)).wait_recv()
        for r in range(2):
            arrive(r, (0, 0))

    loads[0].wait()
    loads[1].wait()
    lane_group = lax.div(lax.rem(lax.broadcasted_iota(jnp.int32, (1, 2 * LANES), 1), LANES), 16)

    def sums_tile(t, carry):
        lanes = pl.ds(pl.multiple_of(t * LANES, LANES), LANES)
        u = (kb[:, lanes].astype(F32) * vb[:, lanes].astype(F32)).astype(BF16)
        ub[:, lanes] = u
        lam = lam_ref[0:1, lanes]
        back = 255.0 - lax.broadcasted_iota(jnp.int32, (SUB, LANES), 0).astype(F32)
        inject = jnp.exp(-lam * back).T.astype(BF16)
        for p in range(2):
            rhs = jnp.concatenate([u[512 * p : 512 * p + 256], u[512 * p + 256 : 512 * p + 512]], axis=1)
            full = jnp.dot(inject, rhs, preferred_element_type=F32)
            total = jnp.zeros((16, 2 * LANES), F32)
            for g in range(8):
                total = jnp.where(lane_group == g, full[16 * g : 16 * g + 16], total)
            bs[2 * p, :, lanes] = total[:, :LANES]
            bs[2 * p + 1, :, lanes] = total[:, LANES:]
        return carry

    lax.fori_loop(0, TILES, sums_tile, 0)

    def decay(steps):
        return jnp.exp(rates_ref[...] * (-steps))

    block_decay = decay(256.0)
    ent[1] = bs[0]
    ent[2] = block_decay * ent[1] + bs[1]
    ent[3] = block_decay * ent[2] + bs[2]
    final = block_decay * ent[3] + bs[3]
    ent[0] = final
    st_send[0] = final.astype(BF16)
    send(st_send.at[0], st_sib, st_sem.at[0, 0], st_sem.at[1, 0], (sib, z))

    weights_start()

    row_i = lax.broadcasted_iota(jnp.int32, (LANES, SUB), 0)
    col_i = lax.broadcasted_iota(jnp.int32, (LANES, SUB), 1)
    above = col_i - row_i > LANES

    def conv_tile(t, carry):
        lanes = pl.ds(pl.multiple_of(t * LANES, LANES), LANES)
        rows = taps_ref[pl.ds(pl.multiple_of(t * 8, 8), 8), :]
        for g in range(8):
            wide = jnp.broadcast_to(rows[g : g + 1, :], (LANES, SUB))
            low = pltpu.roll(wide, 0, 1, stride=1, stride_axis=0)
            low = jnp.where(above, 0.0, low)
            top = jnp.concatenate([low[:, LANES:], jnp.zeros((LANES, LANES), F32)], axis=1)
            band[pl.ds(g * 256, 128), :] = top.astype(BF16)
            band[pl.ds(g * 256 + 128, 128), :] = low.astype(BF16)
        for p in range(2):
            u0 = ub[pl.ds(512 * p, 256), lanes]
            u1 = ub[pl.ds(512 * p + 256, 256), lanes]
            rhs = jnp.concatenate([u0, u1], axis=1)
            local = jnp.zeros((SUB, 2 * LANES), F32)
            for g in range(8):
                part = jnp.dot(band[pl.ds(g * 256, 256), :], rhs, preferred_element_type=F32)
                local = jnp.where(lane_group == g, part, local)
            zloc[pl.ds(512 * p, 256), lanes] = local[:, :LANES]
            zloc[pl.ds(512 * p + 256, 256), lanes] = local[:, LANES:]
        return carry

    def st_wait(buf, i):
        remote(buf, buf, st_sem.at[0, i], st_sem.at[1, i], (s, z)).wait_recv()

    xf, yf = x.astype(F32), y.astype(F32)

    lax.fori_loop(0, 2, conv_tile, 0)

    st_wait(st_sib, 0)
    mine, other = ent[0], st_sib[...].astype(F32)
    first = jnp.where(c == 0, mine, other)
    second = jnp.where(c == 0, other, mine)
    chip_total = decay(1024.0) * first + second
    ent[0] = first
    st_send[1] = chip_total.astype(BF16)
    for d in (1, 3, 2):
        send(st_send.at[1], st_y.at[d - 1], st_sem.at[0, d], st_sem.at[1, d], (at_xy(0, d), z))
    bs[0] = chip_total

    lax.fori_loop(2, 5, conv_tile, 0)
    for r in range(2):
        arrive(r, (1, 0))
        arrive(r, (3, 0))

    row_total = decay(2048.0 * (3.0 - yf)) * bs[0]
    before = jnp.zeros((16, 1024), F32)
    for d in (1, 2, 3):
        st_wait(st_y.at[d - 1], d)
        got = st_y[d - 1].astype(F32)
        from_y = lax.rem(y + 4 - d, 4).astype(F32)
        row_total = row_total + decay(2048.0 * (3.0 - from_y)) * got
        before = before + jnp.where(y >= d, decay(2048.0 * (d - 1)) * got, 0.0)
    st_send[2] = row_total.astype(BF16)
    for d in (1, 3, 2):
        send(st_send.at[2], st_x.at[d - 1], st_sem.at[0, 3 + d], st_sem.at[1, 3 + d], (at_xy(d, 0), z))
    bs[1] = before

    lax.fori_loop(5, TILES, conv_tile, 0)

    far = jnp.zeros((16, 1024), F32)
    for d in (1, 2, 3):
        st_wait(st_x.at[d - 1], 3 + d)
        far = far + jnp.where(x >= d, decay(8192.0 * (d - 1)) * st_x[d - 1].astype(F32), 0.0)
    earlier = bs[1] + decay(2048.0 * yf) * far
    incoming = jnp.where(c == 0, earlier, decay(1024.0) * earlier + ent[0])
    ent[0] = incoming
    for n in range(1, 4):
        ent[n] = ent[n] + decay(256.0 * n) * incoming

    loads[2].wait()
    diag = lax.div(lax.broadcasted_iota(jnp.int32, (LANES, LANES), 0), 16) == lax.div(
        lax.broadcasted_iota(jnp.int32, (LANES, LANES), 1), 16
    )

    def gate(i, n0, n1):
        def gate_tile(t, carry):
            lanes = pl.ds(pl.multiple_of(t * LANES, LANES), LANES)
            lam = lam_ref[0:1, lanes]
            step = lax.broadcasted_iota(jnp.int32, (SUB, LANES), 0).astype(F32) + 1.0
            read = res_ref[0:1, lanes] * jnp.exp(-lam * step)
            read_hi = read.astype(BF16)
            read_lo = (read - read_hi.astype(F32)).astype(BF16)
            his, los = [], []
            for n in (n0, n1):
                e = ent[n, :, lanes]
                e = jnp.where(diag, jnp.concatenate([e] * 8, axis=0), 0.0)
                hi = e.astype(BF16)
                his.append(hi)
                los.append((e - hi.astype(F32)).astype(BF16))
            hi = jnp.concatenate(his, axis=1)
            lo = jnp.concatenate(los, axis=1)
            carried = jnp.dot(
                jnp.concatenate([read_hi, read_hi, read_lo], axis=1),
                jnp.concatenate([hi, lo, hi], axis=0),
                preferred_element_type=F32,
            )
            for k, (n, dst) in enumerate(((n0, send_a.at[i]), (n1, lhs.at[i, par]))):
                rows = pl.ds(pl.multiple_of(n * 256, 256), 256)
                zz = zloc[rows, lanes] + carried[:, k * LANES : (k + 1) * LANES]
                dst[pl.ds(0, 256), lanes] = (qb[rows, lanes].astype(F32) * zz).astype(BF16)
            return carry

        lax.fori_loop(0, TILES, gate_tile, 0)
        send(send_a.at[i], lhs.at[i, par, pl.ds(0, 256)], a_sem.at[0, i], a_sem.at[1, i], (s, z_a))
        send(
            lhs.at[i, par, pl.ds(0, 256)], lhs.at[i, par, pl.ds(256, 256)],
            fwd_sem.at[0, i, 0], fwd_sem.at[1, i, 0], (sib, z),
        )

    gate(0, 3 - z_a, 3 - z)
    gate(1, z_a, z)

    for r in range(2):
        arrive(r, (2, 0))

    def gathered(i):
        ref = lhs.at[i, 1 - par, pl.ds(0, 256)]
        remote(ref, ref, a_sem.at[0, i], a_sem.at[1, i], (s, z_a)).wait_recv()
        send(
            ref, lhs.at[i, 1 - par, pl.ds(256, 256)],
            fwd_sem.at[0, i, 1], fwd_sem.at[1, i, 1], (sib, z),
        )

    def gathered_sib(i):
        for f, h in ((0, par), (1, 1 - par)):
            ref = lhs.at[i, h, pl.ds(256, 256)]
            remote(ref, ref, fwd_sem.at[0, i, f], fwd_sem.at[1, i, f], (sib, z)).wait_recv()

    def multiply(i, j):
        def half(m, carry):
            rows = pl.ds(pl.multiple_of(m * 256, 256), 256)
            left = jnp.concatenate([lhs[i, 0, rows, :], lhs[i, 1, rows, :]], axis=1)
            right = jnp.concatenate(
                [
                    jnp.concatenate([wb[chip(*rel), r, h] for rel in ORDER[2 * j : 2 * j + 2]], axis=1)
                    for h in range(2)
                    for r in range(2)
                ],
                axis=0,
            )
            val = jnp.dot(left, right, preferred_element_type=F32)
            if i == 0:
                send_b[j, rows, :] = val.astype(BF16)
            else:
                acc[j, rows, :] = val
            return carry

        lax.fori_loop(0, 2, half, 0)

    def need(j):
        for dx, dy in ORDER[2 * j : 2 * j + 2]:
            arrive(0, (dx, dy))
            arrive(1, (dy, dx))

    def partial(j):
        need(j)
        multiply(0, j)
        send(send_b.at[j], recv_b.at[j], b_sem.at[0, j], b_sem.at[1, j], (s, z_b))

    outs = []

    def finish(j):
        remote(recv_b.at[j], recv_b.at[j], b_sem.at[0, j], b_sem.at[1, j], (s, z_b)).wait_recv()
        val = (acc[j] + recv_b[j].astype(F32)).astype(BF16)
        for k in range(2):
            cols = pl.ds(pl.multiple_of(chip(*ORDER[2 * j + k]) * 256 + c * 128, 128), 128)
            part = val[:, k * LANES : (k + 1) * LANES]
            stage[j, k, 0] = part[:256]
            stage[j, k, 1] = part[256:]
            cp = pltpu.make_async_copy(stage.at[j, k, 0], out_hbm.at[:, cols], o_sem.at[0, 2 * j + k])
            cp.start()
            outs.append(cp)
            send(
                stage.at[j, k, 1], out_hbm.at[:, cols],
                o_sem.at[1, 2 * j + k], o_sem.at[2, 2 * j + k], (sib, z),
            )

    gathered(0)
    gathered_sib(0)
    partial(0)
    partial(1)
    partial(2)
    gathered(1)
    gathered_sib(1)
    multiply(1, 0)
    for j in range(3, CHUNKS):
        partial(j)
        multiply(1, j - 2)
        finish(j - 3)
    multiply(1, CHUNKS - 2)
    multiply(1, CHUNKS - 1)
    for j in range(CHUNKS - 3, CHUNKS):
        finish(j)

    for j in range(CHUNKS):
        for k in range(2):
            cols = pl.ds(pl.multiple_of(chip(*ORDER[2 * j + k]) * 256 + (1 - c) * 128, 128), 128)
            remote(
                stage.at[j, k, 1], out_hbm.at[:, cols],
                o_sem.at[1, 2 * j + k], o_sem.at[2, 2 * j + k], (sib, z),
            ).wait_recv()
    for cp in outs:
        cp.wait()
    for cp in pending:
        cp.wait_send()


def on_device(query_feat, key_feat, value_feat, decay_rates, residues, out_weight):
    groups = decay_rates.shape[0]
    lag = jnp.mod(128 - jnp.arange(SUB), SUB).astype(F32)
    taps = jnp.sum(residues[:, :, None] * jnp.exp(-decay_rates[:, :, None] * lag), axis=1)
    taps = taps.astype(BF16).astype(F32)
    rates = jnp.repeat(decay_rates.T, 16, axis=1)
    lam = decay_rates.reshape(1, -1)
    res = residues.reshape(1, -1)
    n_w = 2 + 2 * (2 + 2) * 5
    hbm = pl.BlockSpec(memory_space=pl.ANY)
    vmem = pl.BlockSpec(memory_space=pltpu.VMEM)
    return pl.pallas_call(
        kernel,
        out_shape=jax.ShapeDtypeStruct((256, 4096), BF16),
        in_specs=[hbm] * 4 + [vmem] * 4,
        out_specs=hbm,
        scratch_shapes=[
            pltpu.VMEM((1024, 1024), BF16),
            pltpu.VMEM((1024, 1024), BF16),
            pltpu.VMEM((1024, 1024), BF16),
            pltpu.VMEM((1024, 1024), BF16),
            pltpu.VMEM((1024, 1024), F32),
            pltpu.VMEM((2048, 256), BF16),
            pltpu.VMEM((4, 16, 1024), F32),
            pltpu.VMEM((4, 16, 1024), F32),
            pltpu.VMEM((CHIPS, 2, 2, 512, 128), BF16),
            pltpu.VMEM((2, 2, 512, 1024), BF16),
            pltpu.VMEM((2, 256, 1024), BF16),
            pltpu.VMEM((CHUNKS, 512, 256), BF16),
            pltpu.VMEM((CHUNKS, 512, 256), BF16),
            pltpu.VMEM((CHUNKS, 512, 256), F32),
            pltpu.VMEM((CHUNKS, 2, 2, 256, 128), BF16),
            pltpu.VMEM((3, 16, 1024), BF16),
            pltpu.VMEM((16, 1024), BF16),
            pltpu.VMEM((3, 16, 1024), BF16),
            pltpu.VMEM((3, 16, 1024), BF16),
            pltpu.SemaphoreType.DMA((5,)),
            pltpu.SemaphoreType.DMA((1,)),
            pltpu.SemaphoreType.DMA((2, 7)),
            pltpu.SemaphoreType.DMA((n_w,)),
            pltpu.SemaphoreType.DMA((n_w,)),
            pltpu.SemaphoreType.DMA((2, 2)),
            pltpu.SemaphoreType.DMA((2, CHUNKS)),
            pltpu.SemaphoreType.DMA((2, 2, 2)),
            pltpu.SemaphoreType.DMA((3, 2 * CHUNKS)),
        ],
        compiler_params=pltpu.CompilerParams(
            collective_id=0, has_side_effects=True, vmem_limit_bytes=60 * 1024 * 1024
        ),
    )(query_feat, key_feat, value_feat, out_weight, rates, lam, res, taps)


def solution(mesh):
    in_specs = (
        P("seq", "ch"),
        P("seq", "ch"),
        P("seq", "ch"),
        P("ch", None),
        P("ch", None),
        P("ch", "seq"),
    )
    out_specs = P(("seq", "ch"), None)
    return jax.shard_map(
        on_device, mesh=mesh, in_specs=in_specs, out_specs=out_specs, check_vma=False
    )
```

```python
import functools

import jax
import jax.numpy as jnp
from jax import lax
from jax.experimental import pallas as pl
from jax.experimental.pallas import tpu as pltpu
from jax.sharding import PartitionSpec as P

SUB = 256
LANES = 128
TILES = 8
RING = 4
CHIPS = RING * RING
CHUNKS = CHIPS // 2
F32 = jnp.float32
BF16 = jnp.bfloat16
MESH = pl.DeviceIdType.MESH

ORDER = [
    (0, 0), (1, 0), (3, 0), (0, 1), (0, 3), (1, 1), (1, 3), (3, 1),
    (3, 3), (2, 0), (0, 2), (2, 1), (2, 3), (1, 2), (3, 2), (2, 2),
]


def tables(decay_ref, resid_ref, rates_ref, lam_ref, res_ref, taps_ref):
    exact = dict(preferred_element_type=F32, precision=lax.Precision.HIGHEST)
    rate = decay_ref[...]
    resid = resid_ref[...]
    groups = rate.shape[0]
    eye = (
        lax.broadcasted_iota(jnp.int32, (16, 16), 0) == lax.broadcasted_iota(jnp.int32, (16, 16), 1)
    ).astype(F32)
    by_mode = lax.dot_general(eye, rate, (((1,), (1,)), ((), ())), **exact)
    lane = lax.broadcasted_iota(jnp.int32, (groups, 1024), 1)
    own_group = lax.div(lane, 16) == lax.broadcasted_iota(jnp.int32, (groups, 1024), 0)
    rates_ref[...] = jnp.dot(by_mode, own_group.astype(F32), **exact)
    lane16 = lax.broadcasted_iota(jnp.int32, (16, 1024), 1)
    own_mode = (lax.rem(lane16, 16) == lax.broadcasted_iota(jnp.int32, (16, 1024), 0)).astype(F32)
    for table, ref in ((rate, lam_ref), (resid, res_ref)):
        wide = jnp.dot(table, own_mode, **exact)
        ref[...] = jnp.sum(jnp.where(own_group, wide, 0.0), axis=0, keepdims=True)
    lag = lax.rem(128 + SUB - lax.broadcasted_iota(jnp.int32, (1, SUB), 1), SUB).astype(F32)
    total = jnp.zeros((groups, SUB), F32)
    for m in range(16):
        total = total + resid[:, m : m + 1] * jnp.exp(-rate[:, m : m + 1] * lag)
    taps_ref[...] = total.astype(BF16).astype(F32)


def kernel(
    q_hbm, k_hbm, v_hbm, w_hbm, decay_ref, resid_ref, out_hbm,
    qb, kb, vb, ub, zloc, band, bs, ent, wb, lhs, send_a, send_b, recv_b, acc, stage,
    st_send, st_sib, st_y, st_x, rates_ref, lam_ref, res_ref, taps_ref,
    load_sem, sib_sem, st_sem, w_send, w_recv, a_sem, b_sem, fwd_sem, o_sem,
):
    s = lax.axis_index("seq")
    z = lax.axis_index("ch")
    x = lax.div(s, 8)
    y = lax.rem(lax.div(s, 2), 4)
    c = lax.rem(s, 2)
    par = lax.rem(z, 2)
    z_a = z + 1 - 2 * par
    z_b = 3 - z
    sib = s + 1 - 2 * c

    def at_xy(dx, dy):
        return (lax.rem(x + dx, 4) * 4 + lax.rem(y + dy, 4)) * 2 + c

    def chip(dx, dy):
        return lax.rem(x + dx, 4) * 4 + lax.rem(y + dy, 4)

    pending = []

    def remote(src, dst, ssem, rsem, dev):
        return pltpu.make_async_remote_copy(
            src_ref=src, dst_ref=dst, send_sem=ssem, recv_sem=rsem, device_id=dev, device_id_type=MESH
        )

    def send(src, dst, ssem, rsem, dev):
        cp = remote(src, dst, ssem, rsem, dev)
        cp.start()
        pending.append(cp)

    loads = []
    for i, (src, dst) in enumerate(((k_hbm, kb), (v_hbm, vb), (q_hbm, qb))):
        loads.append(pltpu.make_async_copy(src, dst, load_sem.at[i]))
    for r in range(2):
        loads.append(
            pltpu.make_async_copy(w_hbm.at[pl.ds(r * 512, 512), :], wb.at[chip(0, 0), r, par], load_sem.at[3 + r])
        )
    for cp in loads:
        cp.start()

    partners = [(sib, z), (s, z_a), (s, z_b)]
    partners += [(at_xy(d, 0), z) for d in (1, 2, 3)] + [(at_xy(0, d), z) for d in (1, 2, 3)]
    barrier = pltpu.get_barrier_semaphore()
    for dev in partners:
        pl.semaphore_signal(barrier, inc=1, device_id=dev, device_id_type=MESH)
    tables(decay_ref, resid_ref, rates_ref, lam_ref, res_ref, taps_ref)
    pl.semaphore_wait(barrier, len(partners))

    own = chip(0, 0)
    for r in range(2):
        send(w_hbm.at[pl.ds(r * 512, 512), :], wb.at[own, r, par], w_send.at[r], w_recv.at[r], (s, z_a))

    send_slots = {}
    recv_slots = {}

    def slot_of(table, base, key):
        if key not in table:
            table[key] = base + len(table)
        return table[key]

    def to_xy(r, df, dg):
        return (df, dg) if r == 0 else (dg, df)

    def w_copy(r, origin, step, half, key):
        slot = chip(*to_xy(r, *origin))
        ref = wb.at[slot, r] if half is None else wb.at[slot, r, half]
        ss = slot_of(send_slots, 2, (r, origin, step, half))
        rs = slot_of(recv_slots, 2, (r,) + key)
        return remote(ref, ref, w_send.at[ss], w_recv.at[rs], (at_xy(*to_xy(r, *step)), z))

    def w_hop(r, origin, step, half):
        key = ((origin[0] - step[0]) % 4, (origin[1] - step[1]) % 4, half)
        cp = w_copy(r, origin, step, half, key)
        cp.start()
        pending.append(cp)

    def w_wait(r, rel, half):
        slot = chip(*to_xy(r, *rel))
        ref = wb.at[slot, r] if half is None else wb.at[slot, r, half]
        rs = slot_of(recv_slots, 2, (r, rel[0], rel[1], half))
        remote(ref, ref, w_send.at[0], w_recv.at[rs], (s, z)).wait_recv()

    arrived = set()

    def arrive(r, rel):
        if (r, rel) in arrived:
            return
        arrived.add((r, rel))
        df, dg = rel
        if rel == (0, 0):
            w_hop(r, rel, (1, 0), None)
            w_hop(r, rel, (3, 0), None)
            w_hop(r, rel, (0, 1), None)
            w_hop(r, rel, (0, 3), None)
            return
        on_f = dg == 0
        d = df if on_f else dg
        if d == 2:
            w_wait(r, rel, 0)
            w_wait(r, rel, 1)
        else:
            w_wait(r, rel, None)
            fwd = 1 if d == 3 else 3
            w_hop(r, rel, (fwd, 0) if on_f else (0, fwd), 0 if d == 3 else 1)
        if on_f:
            w_hop(r, rel, (0, 1), None)
            w_hop(r, rel, (0, 3), None)

    def weights_start():
        for r in range(2):
            loads[3 + r].wait()
            slab = wb.at[own, r, 1 - par]
            remote(slab, slab, w_send.at[0], w_recv.at[r], (s, z_a)).wait_recv()
        for r in range(2):
            arrive(r, (0, 0))

    loads[0].wait()
    loads[1].wait()
    lane_group = lax.div(lax.rem(lax.broadcasted_iota(jnp.int32, (1, 2 * LANES), 1), LANES), 16)

    def sums_tile(t, carry):
        lanes = pl.ds(pl.multiple_of(t * LANES, LANES), LANES)
        u = (kb[:, lanes].astype(F32) * vb[:, lanes].astype(F32)).astype(BF16)
        ub[:, lanes] = u
        lam = lam_ref[0:1, lanes]
        back = 255.0 - lax.broadcasted_iota(jnp.int32, (SUB, LANES), 0).astype(F32)
        inject = jnp.exp(-lam * back).T.astype(BF16)
        for p in range(2):
            rhs = jnp.concatenate([u[512 * p : 512 * p + 256], u[512 * p + 256 : 512 * p + 512]], axis=1)
            full = jnp.dot(inject, rhs, preferred_element_type=F32)
            total = jnp.zeros((16, 2 * LANES), F32)
            for g in range(8):
                total = jnp.where(lane_group == g, full[16 * g : 16 * g + 16], total)
            bs[2 * p, :, lanes] = total[:, :LANES]
            bs[2 * p + 1, :, lanes] = total[:, LANES:]
        return carry

    lax.fori_loop(0, TILES, sums_tile, 0)

    def decay(steps):
        return jnp.exp(rates_ref[...] * (-steps))

    block_decay = decay(256.0)
    ent[1] = bs[0]
    ent[2] = block_decay * ent[1] + bs[1]
    ent[3] = block_decay * ent[2] + bs[2]
    final = block_decay * ent[3] + bs[3]
    ent[0] = final
    st_send[0] = final.astype(BF16)
    send(st_send.at[0], st_sib, st_sem.at[0, 0], st_sem.at[1, 0], (sib, z))

    row_i = lax.broadcasted_iota(jnp.int32, (LANES, SUB), 0)
    col_i = lax.broadcasted_iota(jnp.int32, (LANES, SUB), 1)
    above = col_i - row_i > LANES

    def conv_tile(t, carry):
        lanes = pl.ds(pl.multiple_of(t * LANES, LANES), LANES)
        rows = taps_ref[pl.ds(pl.multiple_of(t * 8, 8), 8), :]
        for g in range(8):
            wide = jnp.broadcast_to(rows[g : g + 1, :], (LANES, SUB))
            low = pltpu.roll(wide, 0, 1, stride=1, stride_axis=0)
            low = jnp.where(above, 0.0, low)
            top = jnp.concatenate([low[:, LANES:], jnp.zeros((LANES, LANES), F32)], axis=1)
            band[pl.ds(g * 256, 128), :] = top.astype(BF16)
            band[pl.ds(g * 256 + 128, 128), :] = low.astype(BF16)
        for p in range(2):
            u0 = ub[pl.ds(512 * p, 256), lanes]
            u1 = ub[pl.ds(512 * p + 256, 256), lanes]
            rhs = jnp.concatenate([u0, u1], axis=1)
            local = jnp.zeros((SUB, 2 * LANES), F32)
            for g in range(8):
                part = jnp.dot(band[pl.ds(g * 256, 256), :], rhs, preferred_element_type=F32)
                local = jnp.where(lane_group == g, part, local)
            zloc[pl.ds(512 * p, 256), lanes] = local[:, :LANES]
            zloc[pl.ds(512 * p + 256, 256), lanes] = local[:, LANES:]
        return carry

    def st_wait(buf, i):
        remote(buf, buf, st_sem.at[0, i], st_sem.at[1, i], (s, z)).wait_recv()

    xf, yf = x.astype(F32), y.astype(F32)

    lax.fori_loop(0, 2, conv_tile, 0)

    st_wait(st_sib, 0)
    mine, other = ent[0], st_sib[...].astype(F32)
    first = jnp.where(c == 0, mine, other)
    second = jnp.where(c == 0, other, mine)
    chip_total = decay(1024.0) * first + second
    ent[0] = first
    st_send[1] = chip_total.astype(BF16)
    for d in (1, 3, 2):
        send(st_send.at[1], st_y.at[d - 1], st_sem.at[0, d], st_sem.at[1, d], (at_xy(0, d), z))
    bs[0] = chip_total

    weights_start()
    lax.fori_loop(2, 5, conv_tile, 0)

    row_total = decay(2048.0 * (3.0 - yf)) * bs[0]
    before = jnp.zeros((16, 1024), F32)
    for d in (1, 2, 3):
        st_wait(st_y.at[d - 1], d)
        got = st_y[d - 1].astype(F32)
        from_y = lax.rem(y + 4 - d, 4).astype(F32)
        row_total = row_total + decay(2048.0 * (3.0 - from_y)) * got
        before = before + jnp.where(y >= d, decay(2048.0 * (d - 1)) * got, 0.0)
    st_send[2] = row_total.astype(BF16)
    for d in (1, 3, 2):
        send(st_send.at[2], st_x.at[d - 1], st_sem.at[0, 3 + d], st_sem.at[1, 3 + d], (at_xy(d, 0), z))
    bs[1] = before

    lax.fori_loop(5, TILES, conv_tile, 0)
    for r in range(2):
        arrive(r, (1, 0))
        arrive(r, (3, 0))

    far = jnp.zeros((16, 1024), F32)
    for d in (1, 2, 3):
        st_wait(st_x.at[d - 1], 3 + d)
        far = far + jnp.where(x >= d, decay(8192.0 * (d - 1)) * st_x[d - 1].astype(F32), 0.0)
    earlier = bs[1] + decay(2048.0 * yf) * far
    incoming = jnp.where(c == 0, earlier, decay(1024.0) * earlier + ent[0])
    ent[0] = incoming
    for n in range(1, 4):
        ent[n] = ent[n] + decay(256.0 * n) * incoming

    loads[2].wait()
    diag = lax.div(lax.broadcasted_iota(jnp.int32, (LANES, LANES), 0), 16) == lax.div(
        lax.broadcasted_iota(jnp.int32, (LANES, LANES), 1), 16
    )

    def gate(i, half, n0, n1):
        first_row = half * 128

        def gate_tile(t, carry):
            lanes = pl.ds(pl.multiple_of(t * LANES, LANES), LANES)
            lam = lam_ref[0:1, lanes]
            step = lax.broadcasted_iota(jnp.int32, (128, LANES), 0).astype(F32) + (first_row + 1.0)
            read = res_ref[0:1, lanes] * jnp.exp(-lam * step)
            read_hi = read.astype(BF16)
            read_lo = (read - read_hi.astype(F32)).astype(BF16)
            his, los = [], []
            for n in (n0, n1):
                e = ent[n, :, lanes]
                e = jnp.where(diag, jnp.concatenate([e] * 8, axis=0), 0.0)
                hi = e.astype(BF16)
                his.append(hi)
                los.append((e - hi.astype(F32)).astype(BF16))
            hi = jnp.concatenate(his, axis=1)
            lo = jnp.concatenate(los, axis=1)
            carried = jnp.dot(
                jnp.concatenate([read_hi, read_hi, read_lo], axis=1),
                jnp.concatenate([hi, lo, hi], axis=0),
                preferred_element_type=F32,
            )
            for k, (n, dst) in enumerate(((n0, send_a.at[i, half]), (n1, lhs.at[i, half, par]))):
                rows = pl.ds(pl.multiple_of(n * 256 + first_row, 128), 128)
                zz = zloc[rows, lanes] + carried[:, k * LANES : (k + 1) * LANES]
                dst[pl.ds(0, 128), lanes] = (qb[rows, lanes].astype(F32) * zz).astype(BF16)
            return carry

        lax.fori_loop(0, TILES, gate_tile, 0)
        send(
            send_a.at[i, half], lhs.at[i, half, par, pl.ds(0, 128)],
            a_sem.at[0, i, half], a_sem.at[1, i, half], (s, z_a),
        )
        send(
            lhs.at[i, half, par, pl.ds(0, 128)], lhs.at[i, half, par, pl.ds(128, 128)],
            fwd_sem.at[0, i, half, 0], fwd_sem.at[1, i, half, 0], (sib, z),
        )

    gate(0, 0, 3 - z_a, 3 - z)
    gate(0, 1, 3 - z_a, 3 - z)
    for r in range(2):
        arrive(r, (0, 1))
        arrive(r, (0, 3))
    gate(1, 0, z_a, z)
    gate(1, 1, z_a, z)
    for r in range(2):
        arrive(r, (2, 0))

    def gathered(i, half):
        ref = lhs.at[i, half, 1 - par, pl.ds(0, 128)]
        remote(ref, ref, a_sem.at[0, i, half], a_sem.at[1, i, half], (s, z_a)).wait_recv()
        send(
            ref, lhs.at[i, half, 1 - par, pl.ds(128, 128)],
            fwd_sem.at[0, i, half, 1], fwd_sem.at[1, i, half, 1], (sib, z),
        )

    def gathered_sib(i, half):
        for f, h in ((0, par), (1, 1 - par)):
            ref = lhs.at[i, half, h, pl.ds(128, 128)]
            remote(ref, ref, fwd_sem.at[0, i, half, f], fwd_sem.at[1, i, half, f], (sib, z)).wait_recv()

    def multiply(i, half, j):
        left = jnp.concatenate([lhs[i, half, 0], lhs[i, half, 1]], axis=1)
        right = jnp.concatenate(
            [
                jnp.concatenate([wb[chip(*rel), r, h] for rel in ORDER[2 * j : 2 * j + 2]], axis=1)
                for h in range(2)
                for r in range(2)
            ],
            axis=0,
        )
        return jnp.dot(left, right, preferred_element_type=F32)

    def need(j):
        for dx, dy in ORDER[2 * j : 2 * j + 2]:
            arrive(0, (dx, dy))
            arrive(1, (dy, dx))

    def partial(j, half):
        need(j)
        send_b[j, half] = multiply(0, half, j).astype(BF16)
        send(send_b.at[j, half], recv_b.at[j, half], b_sem.at[0, j, half], b_sem.at[1, j, half], (s, z_b))

    def keep(j, half):
        acc[j, half] = multiply(1, half, j)

    outs = []

    def finish(j, half):
        ref = recv_b.at[j, half]
        remote(ref, ref, b_sem.at[0, j, half], b_sem.at[1, j, half], (s, z_b)).wait_recv()
        val = (acc[j, half] + recv_b[j, half].astype(F32)).astype(BF16)
        for k in range(2):
            cols = pl.ds(pl.multiple_of(chip(*ORDER[2 * j + k]) * 256 + c * 128, 128), 128)
            part = val[:, k * LANES : (k + 1) * LANES]
            stage[j, half, k, 0] = part[:128]
            stage[j, half, k, 1] = part[128:]
            place = out_hbm.at[pl.ds(half * 128, 128), cols]
            cp = pltpu.make_async_copy(stage.at[j, half, k, 0], place, o_sem.at[0, 2 * j + k, half])
            cp.start()
            outs.append(cp)
            send(
                stage.at[j, half, k, 1], place,
                o_sem.at[1, 2 * j + k, half], o_sem.at[2, 2 * j + k, half], (sib, z),
            )

    gathered(0, 0)
    gathered_sib(0, 0)
    partial(0, 0)
    partial(1, 0)
    gathered(0, 1)
    gathered_sib(0, 1)
    partial(0, 1)
    partial(1, 1)
    gathered(1, 0)
    partial(2, 0)
    partial(2, 1)
    gathered(1, 1)
    partial(3, 0)
    partial(3, 1)
    gathered_sib(1, 0)
    gathered_sib(1, 1)
    for j in range(4, CHUNKS):
        for half in range(2):
            partial(j, half)
            keep(j - 4, half)
            finish(j - 4, half)
    for j in range(CHUNKS - 4, CHUNKS):
        for half in range(2):
            keep(j, half)
    for j in range(CHUNKS - 4, CHUNKS):
        for half in range(2):
            finish(j, half)

    for j in range(CHUNKS):
        for half in range(2):
            for k in range(2):
                cols = pl.ds(pl.multiple_of(chip(*ORDER[2 * j + k]) * 256 + (1 - c) * 128, 128), 128)
                remote(
                    stage.at[j, half, k, 1], out_hbm.at[pl.ds(half * 128, 128), cols],
                    o_sem.at[1, 2 * j + k, half], o_sem.at[2, 2 * j + k, half], (sib, z),
                ).wait_recv()
    for cp in outs:
        cp.wait()
    for cp in pending:
        cp.wait_send()


def on_device(query_feat, key_feat, value_feat, decay_rates, residues, out_weight):
    n_w = 2 + 2 * (2 + 2) * 5
    hbm = pl.BlockSpec(memory_space=pl.ANY)
    vmem = pl.BlockSpec(memory_space=pltpu.VMEM)
    return pl.pallas_call(
        kernel,
        out_shape=jax.ShapeDtypeStruct((256, 4096), BF16),
        in_specs=[hbm] * 4 + [vmem] * 2,
        out_specs=hbm,
        scratch_shapes=[
            pltpu.VMEM((1024, 1024), BF16),
            pltpu.VMEM((1024, 1024), BF16),
            pltpu.VMEM((1024, 1024), BF16),
            pltpu.VMEM((1024, 1024), BF16),
            pltpu.VMEM((1024, 1024), F32),
            pltpu.VMEM((2048, 256), BF16),
            pltpu.VMEM((4, 16, 1024), F32),
            pltpu.VMEM((4, 16, 1024), F32),
            pltpu.VMEM((CHIPS, 2, 2, 512, 128), BF16),
            pltpu.VMEM((2, 2, 2, 256, 1024), BF16),
            pltpu.VMEM((2, 2, 128, 1024), BF16),
            pltpu.VMEM((CHUNKS, 2, 256, 256), BF16),
            pltpu.VMEM((CHUNKS, 2, 256, 256), BF16),
            pltpu.VMEM((CHUNKS, 2, 256, 256), F32),
            pltpu.VMEM((CHUNKS, 2, 2, 2, 128, 128), BF16),
            pltpu.VMEM((3, 16, 1024), BF16),
            pltpu.VMEM((16, 1024), BF16),
            pltpu.VMEM((3, 16, 1024), BF16),
            pltpu.VMEM((3, 16, 1024), BF16),
            pltpu.VMEM((16, 1024), F32),
            pltpu.VMEM((1, 1024), F32),
            pltpu.VMEM((1, 1024), F32),
            pltpu.VMEM((64, 256), F32),
            pltpu.SemaphoreType.DMA((5,)),
            pltpu.SemaphoreType.DMA((1,)),
            pltpu.SemaphoreType.DMA((2, 7)),
            pltpu.SemaphoreType.DMA((n_w,)),
            pltpu.SemaphoreType.DMA((n_w,)),
            pltpu.SemaphoreType.DMA((2, 2, 2)),
            pltpu.SemaphoreType.DMA((2, CHUNKS, 2)),
            pltpu.SemaphoreType.DMA((2, 2, 2, 2)),
            pltpu.SemaphoreType.DMA((3, 2 * CHUNKS, 2)),
        ],
        compiler_params=pltpu.CompilerParams(
            collective_id=0, has_side_effects=True, vmem_limit_bytes=60 * 1024 * 1024
        ),
    )(query_feat, key_feat, value_feat, out_weight, decay_rates, residues)


def solution(mesh):
    in_specs = (
        P("seq", "ch"),
        P("seq", "ch"),
        P("seq", "ch"),
        P("ch", None),
        P("ch", None),
        P("ch", "seq"),
    )
    out_specs = P(("seq", "ch"), None)
    return jax.shard_map(
        on_device, mesh=mesh, in_specs=in_specs, out_specs=out_specs, check_vma=False
    )
```
